32 devices in a mesh: mx: 8 (over z, core), my: 4 (over y, x).
Axes of the slice: x: 2, y: 2, z: 4, core: 2. Of those that a mesh axis runs over, the one named last changes fastest.
Arguments:
- features: bfloat16 [1024, 32, 512], P(('mx', 'my')), may hold values from -6 to 6
- coords: int32 [3, 1024], P(None, ('mx', 'my')), may hold values from 0 to 31, as said below
- counts: int32 [32], P(('mx', 'my')), may hold values from 16 to 32, as said below
- neighbours: int32 [6, 1024], P(None, ('mx', 'my')), may hold values from -1 to 1023, as said below
- fine_weights: bfloat16 [3, 32, 224], replicated, may hold values from -0.375 to 0.375
- down_weight: bfloat16 [2048, 256], replicated, may hold values from -0.25 to 0.25
- up_weight: bfloat16 [256, 2048], replicated, may hold values from -0.375 to 0.375
- norm_gain: float32 [256], replicated, may hold values from 0.1 to 1.9
- norm_bias: float32 [256], replicated, may hold values from -3 to 3
- coarse_weight: bfloat16 [6912, 256], P(None, 'my'), may hold values from -0.078125 to 0.078125
Outputs:
- fine_out: bfloat16 [1024, 32, 512], P(('mx', 'my'))
- coarse_out: bfloat16 [16, 8, 2, 256], P('mx', 'my')
The draws below stay inside these ranges and needn't reach their ends.
Inputs may be any that keep to these rules, and one draw needn't show every extreme that they name: The live slots of a device are its first counts entries; some device is full in every draw. `coords`: the live blocks of the device with mx index i and my index j lie at z in [i * 4, (i + 1) * 4), y in [j * 4, (j + 1) * 4), x in [0, 4), distinct, in Morton order of their coordinates inside that region; slots that are not live hold 0. `neighbours`: A live block's entry is the slot of the live block one step away in that direction, or -1 if there is none; the relation is symmetric; slots that are not live hold -1.
All inputs are finite; a program needn't handle non-finite values.
Results may differ from the reference program's by a relative error of at most 0.0095.
Values may be sent and summed in bfloat16 or wider, within the bound.
A program may use at most 128 MiB of HBM per device.

```python
import jax
import jax.numpy as jnp
from jax import lax

C = 32
CC = 256
GROUPS = 32
SIDE = 8
RZ = 4
RY = 4
RX = 4
BLK_DEV = 32
SLOTS = 1024
N_MX = 8
N_MY = 4


def morton_code(local_z, local_y, local_x):
    morton = jnp.zeros_like(local_x)
    for bit_pos in range(8):
        morton = morton | (local_x >> bit_pos & 1) << 3 * bit_pos
        morton = morton | (local_y >> bit_pos & 1) << 3 * bit_pos + 1
        morton = morton | (local_z >> bit_pos & 1) << 3 * bit_pos + 2
    return morton


def geometry(key):
    device_total = N_MX * N_MY
    region = RZ * RY * RX
    folded = jax.random.fold_in(key, 11)
    count_key, full_key, choose_key = jax.random.split(folded, 3)
    counts = jax.random.randint(count_key, (device_total,), BLK_DEV // 2, BLK_DEV + 1, dtype=jnp.int32)
    fullest = jax.random.randint(full_key, (), 0, device_total, dtype=jnp.int32)
    device_ids = jnp.arange(device_total, dtype=jnp.int32)
    counts = jnp.where(device_ids == fullest, BLK_DEV, counts).astype(jnp.int32)
    cell_ids = jnp.arange(region, dtype=jnp.int32)
    local_z = cell_ids // (RY * RX)
    local_y = cell_ids // RX % RY
    local_x = cell_ids % RX
    morton = morton_code(local_z, local_y, local_x)

    def per_device(device_key, live_count):
        ranking = jax.random.permutation(device_key, region).astype(jnp.int32)
        chosen = ranking < live_count
        scores = jnp.where(chosen, morton, morton + (1 << 25))
        return jnp.argsort(scores)[:BLK_DEV].astype(jnp.int32)
    orderings = jax.vmap(per_device)(jax.random.split(choose_key, device_total), counts)
    is_live = jnp.arange(BLK_DEV, dtype=jnp.int32)[None, :] < counts[:, None]
    block_z = (device_ids // N_MY)[:, None] * RZ + local_z[orderings]
    block_y = (device_ids % N_MY)[:, None] * RY + local_y[orderings]
    block_x = local_x[orderings]
    block_z = jnp.where(is_live, block_z, 0).reshape(-1)
    block_y = jnp.where(is_live, block_y, 0).reshape(-1)
    block_x = jnp.where(is_live, block_x, 0).reshape(-1)
    is_live = is_live.reshape(-1)
    extent_z = RZ * N_MX
    extent_y = RY * N_MY
    grid_cells = extent_z * extent_y * RX
    linear = (block_z * extent_y + block_y) * RX + block_x
    slot_ids = jnp.arange(device_total * BLK_DEV, dtype=jnp.int32)
    lookup = jnp.full((grid_cells,), -1, jnp.int32).at[jnp.where(is_live, linear, grid_cells)].set(slot_ids, mode='drop')
    steps_list = ((0, 0, 1), (0, 0, -1), (0, 1, 0), (0, -1, 0), (1, 0, 0), (-1, 0, 0))
    link_rows = []
    for step_z, step_y, step_x in steps_list:
        near_z = block_z + step_z
        near_y = block_y + step_y
        near_x = block_x + step_x
        inside = (near_z >= 0) & (near_z < extent_z) & (near_y >= 0) & (near_y < extent_y) & (near_x >= 0) & (near_x < RX) & is_live
        near_linear = (near_z * extent_y + near_y) * RX + near_x
        link_rows.append(jnp.where(inside, lookup[jnp.clip(near_linear, 0, grid_cells - 1)], -1))
    neighbours = jnp.stack(link_rows).astype(jnp.int32)
    coords = jnp.stack([block_z, block_y, block_x]).astype(jnp.int32)
    return (counts, coords, neighbours)


def draw_counts(key, part):
    return geometry(key)[0]


def draw_coords(key, part):
    return geometry(key)[1]


def draw_neighbours(key, part):
    return geometry(key)[2]


def block_levels(rng, shape, cuts, low, top_value):
    def one(position, blocks):
        draws = jax.random.uniform(jax.random.fold_in(jax.random.fold_in(rng, 6), position), (blocks,), jnp.float32, low / len(cuts), top_value / len(cuts))
        return jnp.repeat(jnp.exp(draws), shape[position] // blocks).reshape((-1,) + (1,) * (len(shape) - position - 1))

    level = one(*cuts[0])
    for cut in cuts[1:]:
        level = level * one(*cut)
    return level


def normal_values(own_key, shape, width, most, cuts=(), kind=jnp.bfloat16):
    array = width * jax.random.normal(own_key, shape, jnp.float32)
    if cuts:
        array = array * block_levels(own_key, shape, cuts, -0.22, 0.18)
    return jnp.clip(array, -most, most).astype(kind)


def setup_inputs(seed: int = 0) -> dict:
    splits = jax.random.split(jax.random.key(seed), 11)
    return {
        "features": normal_values(splits[0], (SLOTS, C, SIDE * SIDE * SIDE), 1.0, 6.0, ((0, 32),)),
        "coords": draw_coords(jax.random.fold_in(splits[10], 71), 0),
        "counts": draw_counts(jax.random.fold_in(splits[10], 71), 0),
        "neighbours": draw_neighbours(jax.random.fold_in(splits[10], 71), 0),
        "fine_weights": normal_values(splits[4], (3, C, 7 * C), (7 * C) ** -0.5, 0.375),
        "down_weight": normal_values(splits[5], (64 * C, CC), (16 * C) ** -0.5, 0.25),
        "up_weight": normal_values(splits[6], (CC, 64 * C), CC ** -0.5, 0.375),
        "norm_gain": jnp.clip(1.0 + 0.18 * jax.random.normal(splits[7], (CC,), jnp.float32), 0.1, 1.9),
        "norm_bias": normal_values(splits[8], (CC,), 0.5, 3.0, (), jnp.float32),
        "coarse_weight": normal_values(splits[9], (27 * CC, CC), (27 * CC) ** -0.5, 0.078125, ((1, 4),)),
    }


def displaced_taps(signal, near_blocks, block_side):
    volume = block_side * block_side * block_side
    voxel_ids = jnp.arange(volume, dtype=jnp.int32)
    along_x = voxel_ids % block_side
    along_y = voxel_ids // block_side % block_side
    along_z = voxel_ids // (block_side * block_side)
    last_layer = block_side - 1
    square = block_side * block_side
    plans = ((along_x < last_layer, -1, last_layer), (along_x > 0, 1, -last_layer), (along_y < last_layer, -block_side, block_side * last_layer), (along_y > 0, block_side, -block_side * last_layer), (along_z < last_layer, -square, square * last_layer), (along_z > 0, square, -square * last_layer))
    tap_list = [signal]
    for (inside, own_shift, near_shift), block in zip(plans, near_blocks):
        tap_list.append(jnp.where(inside, jnp.roll(signal, own_shift, axis=2), jnp.roll(block, near_shift, axis=2)))
    tap_stack = jnp.stack(tap_list, axis=1)
    return tap_stack.reshape(signal.shape[0], 7 * signal.shape[1], volume)

def coarse_patches(padded, depth, height, breadth):
    channel_count = padded.shape[3]
    pieces = []
    for step_z in range(3):
        for step_y in range(3):
            for step_x in range(3):
                pieces.append(padded[step_z:step_z + depth, step_y:step_y + height, step_x:step_x + breadth])
    return jnp.stack(pieces, axis=3).reshape(depth * height * breadth, 27 * channel_count)

def residual_step(base, neighbours, kernel_weight):
    signal = jax.nn.silu(base.astype(jnp.float32)).astype(jnp.bfloat16)
    device_total = N_MX * N_MY
    slot_total, chans, volume = base.shape
    block_count = slot_total // device_total

    def per_device(device_id):
        first_row = device_id * block_count
        own_rows = lax.dynamic_slice_in_dim(signal, first_row, block_count, 0)
        kept_rows = lax.dynamic_slice_in_dim(base, first_row, block_count, 0)
        link_rows = lax.dynamic_slice_in_dim(neighbours, first_row, block_count, 1)
        near_blocks = []
        for direction in range(6):
            present = link_rows[direction] >= 0
            picked = signal[jnp.clip(link_rows[direction], 0, slot_total - 1)]
            near_blocks.append(jnp.where(present[:, None, None], picked, jnp.zeros_like(picked)))
        tap_stack = displaced_taps(own_rows, near_blocks, SIDE)
        convolution_result = jnp.einsum('pn,enh->eph', kernel_weight.astype(jnp.float32), tap_stack.astype(jnp.float32))
        return (kept_rows.astype(jnp.float32) + convolution_result).astype(jnp.bfloat16)
    result = lax.map(per_device, jnp.arange(device_total, dtype=jnp.int32))
    return result.reshape(slot_total, chans, volume)

def reference(features, coords, counts, neighbours, fine_weights, down_weight, up_weight, norm_gain, norm_bias, coarse_weight):
    device_total = N_MX * N_MY
    slot_total, chans, volume = features.shape
    block_count = slot_total // device_total
    slot_ids = jnp.arange(slot_total, dtype=jnp.int32)
    is_live = slot_ids % block_count < counts[slot_ids // block_count]
    first_level = residual_step(features, neighbours, fine_weights[0])
    half_side = SIDE // 2
    pooled = lax.optimization_barrier(jnp.mean(first_level.reshape(slot_total, chans, 2, half_side, 2, half_side, 2, half_side), axis=(3, 5, 7), dtype=jnp.float32))
    pooled = pooled.transpose(0, 2, 3, 4, 1).reshape(slot_total, 8 * chans).astype(jnp.bfloat16)
    grid_z = RZ // 2 * N_MX
    grid_y = RY // 2 * N_MY
    grid_x = RX // 2
    cell_count = grid_z * grid_y * grid_x
    block_z = coords[0]
    block_y = coords[1]
    block_x = coords[2]
    cell_ids = (block_z // 2 * grid_y + block_y // 2) * grid_x + block_x // 2
    octant_pos = block_z % 2 * 4 + block_y % 2 * 2 + block_x % 2
    target = jnp.where(is_live, cell_ids * 8 + octant_pos, cell_count * 8).astype(jnp.int32)
    gathered = jnp.zeros((cell_count * 8, 8 * chans), jnp.bfloat16).at[target].set(pooled, mode='drop')
    coarse_in = jnp.dot(gathered.reshape(cell_count, 64 * chans), down_weight, preferred_element_type=jnp.float32)
    coarse_width = coarse_in.shape[1]
    grouped = coarse_in.reshape(cell_count, GROUPS, coarse_width // GROUPS)
    group_mean = lax.optimization_barrier(jnp.mean(grouped, axis=(0, 2)))
    centred = grouped - group_mean[None, :, None]
    variance = lax.optimization_barrier(jnp.mean(centred * centred, axis=(0, 2)))
    normed = (centred / jnp.sqrt(variance + 1e-05)[None, :, None]).reshape(cell_count, coarse_width) * norm_gain + norm_bias
    activated = jax.nn.silu(normed).astype(jnp.bfloat16).reshape(grid_z, grid_y, grid_x, coarse_width)
    padded = jnp.pad(activated, ((1, 1), (1, 1), (1, 1), (0, 0)))
    convolution_result = jnp.dot(coarse_patches(padded, grid_z, grid_y, grid_x), coarse_weight, preferred_element_type=jnp.float32)
    coarse_out = (convolution_result + coarse_in).astype(jnp.bfloat16)
    lifted = jnp.dot(coarse_out, up_weight, preferred_element_type=jnp.float32).reshape(cell_count * 8, 8 * chans)
    per_block = lifted[jnp.clip(target, 0, cell_count * 8 - 1)]
    per_block = jnp.where(is_live[:, None], per_block, jnp.zeros_like(per_block))

    def join_device(device_id):
        first_row = device_id * block_count
        level_row_list = lax.dynamic_slice_in_dim(first_level, first_row, block_count, 0)
        lift_rows = lax.dynamic_slice_in_dim(per_block, first_row, block_count, 0)
        spread_up = lift_rows.reshape(block_count, 2, 2, 2, chans).transpose(0, 4, 1, 2, 3)
        spread_up = jnp.broadcast_to(spread_up[:, :, :, None, :, None, :, None], (block_count, chans, 2, half_side, 2, half_side, 2, half_side))
        return (level_row_list.astype(jnp.float32) + spread_up.reshape(block_count, chans, volume)).astype(jnp.bfloat16)
    merged_features = lax.map(join_device, jnp.arange(device_total, dtype=jnp.int32)).reshape(slot_total, chans, volume)
    second_level = residual_step(merged_features, neighbours, fine_weights[1])
    final_level = residual_step(second_level, neighbours, fine_weights[2])
    fine_out = jnp.where(is_live[:, None, None], final_level, jnp.zeros_like(final_level))
    return (fine_out, coarse_out.reshape(grid_z, grid_y, grid_x, coarse_width))
```

```python
import functools

import jax
import jax.numpy as jnp
import numpy as np
from jax import lax
from jax.experimental import pallas as pl
from jax.experimental.pallas import tpu as pltpu
from jax.sharding import PartitionSpec as P

GROUPS = 32
SIDE = 8
RZ = 4
RY = 4
RX = 4
VOL = SIDE**3
SQ = SIDE * SIDE
NPOS = 16
norm_eps = 1e-05
MESH = pl.DeviceIdType.MESH
BF = jnp.bfloat16
F32 = jnp.float32
VM = pl.BlockSpec(memory_space=pltpu.VMEM)
SM = pl.BlockSpec(memory_space=pltpu.SMEM)


def constants(chans):
    v = np.arange(VOL)
    x, y, z = v % SIDE, v // SIDE % SIDE, v // SQ
    last = SIDE - 1
    masks = np.stack([x < last, x > 0, y < last, y > 0, z < last, z > 0])
    masks = np.broadcast_to(masks[:, None, :], (6, chans, VOL)).astype(np.float32)
    where = (y == 0, y == last, z == 0, z == last)
    spot = (z * SIDE + x, z * SIDE + x, y * SIDE + x, y * SIDE + x)
    sel = np.zeros((4, 2 * VOL, 2 * SQ), np.float32)
    for f in range(4):
        hit = np.nonzero(where[f])[0]
        sel[f, hit, spot[f][hit]] = 1
        sel[f, VOL + hit, SQ + spot[f][hit]] = 1
    half = SIDE // 2
    octant = z // half * 4 + y // half * 2 + x // half
    pool = (octant[None, :] == np.arange(8)[:, None]) / float(half**3)
    lanes = np.arange(8 * chans)
    spread = (np.arange(chans)[:, None] == lanes[None, :] % chans).astype(np.float32)
    octs = (lanes[:, None] // chans == octant[None, :]).astype(np.float32)
    as_bf = lambda a: jnp.asarray(a, BF)
    return as_bf(masks), as_bf(sel), as_bf(pool), as_bf(spread), as_bf(octs)


def silu(x):
    return x * jax.nn.sigmoid(x)


def face_slot(slot_at, face, k):
    a, b = k // 4, k % 4
    if face == 0:
        p = (a * RY + 0) * RX + b
    elif face == 1:
        p = (a * RY + RY - 1) * RX + b
    elif face == 2:
        p = (0 * RY + a) * RX + b
    else:
        p = ((RZ - 1) * RY + a) * RX + b
    return slot_at[p]


def pack_faces(slot_at, ext, sel, faces, stage, chans):
    for f in range(4):
        for k in range(NPOS):
            s = face_slot(slot_at, f, k)
            stage[k // 2 * chans : (k // 2 + 1) * chans, k % 2 * VOL : (k % 2 + 1) * VOL] = ext[s]
        packed = jnp.dot(stage[...], sel[f], preferred_element_type=F32)
        faces[f] = packed.astype(BF)


def unpack_faces(ext, halo, sel, stage, slots, chans):
    for f in range(4):
        wide = lax.dot_general(
            halo[f], sel[f], (((1,), (1,)), ((), ())), preferred_element_type=F32
        ).astype(BF)
        stage[...] = wide
        for k in range(NPOS):
            ext[slots + 1 + f * NPOS + k] = stage[
                k // 2 * chans : (k // 2 + 1) * chans, k % 2 * VOL : (k % 2 + 1) * VOL
            ]


SHIFTS = ((-1, 7), (1, -7), (-8, 56), (8, -56), (-64, 448), (64, -448))


def conv_slot(j, nb, ext, masks, weight):
    own = ext[j]
    taps = [own]
    for d, (a, b) in enumerate(SHIFTS):
        near = ext[nb[d, j]]
        taps.append(
            jnp.where(
                masks[d] > 0.5,
                pltpu.roll(own, a % VOL, 1),
                pltpu.roll(near, b % VOL, 1),
            )
        )
    return jnp.dot(weight, jnp.concatenate(taps, axis=0), preferred_element_type=F32)


def first_faces(slots, chans, slot_at, feat, sel, sig, faces, ext, stage):
    ext[slots] = jnp.zeros((chans, VOL), BF)

    def step(j, c):
        s = silu(feat[j].astype(F32)).astype(BF)
        ext[j] = s
        sig[j] = s
        return c

    lax.fori_loop(0, slots, step, 0, unroll=2)
    pack_faces(slot_at, ext, sel, faces, stage, chans)


def conv_pool(
    slots, chans, cells, slot_at, nb, feat, sig, halo, sel, masks, weight, pool, spread, down,
    level, coarse, stats, ext, stage, pooled, rows,
):
    ext[0:slots] = sig[...]
    ext[slots] = jnp.zeros((chans, VOL), BF)
    unpack_faces(ext, halo, sel, stage, slots, chans)
    pooled[slots] = jnp.zeros((8, chans), F32)
    w = weight[...]
    pm = pool[...]

    def step(j, c):
        f = (feat[j].astype(F32) + conv_slot(j, nb, ext, masks, w)).astype(BF)
        level[j] = f
        pooled[j] = lax.dot_general(pm, f, (((1,), (1,)), ((), ())), preferred_element_type=F32)
        return c

    lax.fori_loop(0, slots, step, 0, unroll=2)
    for p in range(8):
        for q in range(cells):
            z = q // 4 * 2 + p // 4
            x = q // 2 % 2 * 2 + p % 2
            y = q % 2 * 2 + p // 2 % 2
            i = p * cells + q
            rows[i * 8 : (i + 1) * 8, :] = pooled[slot_at[(z * RY + y) * RX + x]]
    wide = jnp.dot(rows[...].astype(BF), spread[...], preferred_element_type=F32)
    n = 8 * cells
    width = 8 * chans
    oct_row = lax.broadcasted_iota(jnp.int32, (n * 8, width), 0) % 8
    oct_lane = lax.broadcasted_iota(jnp.int32, (n * 8, width), 1) // chans
    wide = jnp.where(oct_row == oct_lane, wide, 0.0)
    flat = jnp.sum(wide.reshape(n, 8, width), axis=1).astype(BF)
    acc = jnp.zeros(coarse.shape, F32)
    for p in range(8):
        acc = acc + jnp.dot(
            flat[p * cells : (p + 1) * cells],
            down[p * width : (p + 1) * width, :],
            preferred_element_type=F32,
        )
    coarse[...] = acc
    stats[0:1, :] = jnp.sum(acc, axis=0, keepdims=True)
    stats[1:2, :] = jnp.sum(acc * acc, axis=0, keepdims=True)


def coarse_part(n_my, total, stats, window, gain, bias, weight, part, pad):
    n_mx = lax.axis_size("mx")
    mx = lax.axis_index("mx")
    width = gain.shape[1]
    group = width // GROUPS
    sums = jnp.sum(stats[...], axis=0)
    same = (
        lax.broadcasted_iota(jnp.int32, (width, width), 0) // group
        == lax.broadcasted_iota(jnp.int32, (width, width), 1) // group
    ).astype(F32)
    sums = jnp.concatenate([sums, jnp.zeros((6, width), F32)], axis=0)
    sums = jnp.dot(sums, same, precision=lax.Precision.HIGHEST, preferred_element_type=F32) / total
    mean = sums[0:1]
    std = jnp.sqrt(sums[1:2] - mean * mean + norm_eps)
    g = gain[...]
    b = bias[...]
    pad[...] = jnp.zeros_like(pad)
    for zw in range(4):
        for x in range(2):
            for j in range(n_my):
                value = silu((window[j, zw, x] - mean) / std * g + b)
                if zw == 0:
                    value = jnp.where(mx > 0, value, 0.0)
                if zw == 3:
                    value = jnp.where(mx < n_mx - 1, value, 0.0)
                pad[1 + x, zw, 1 + 2 * j : 3 + 2 * j, :] = value
    tall = 2 * n_my
    acc = jnp.zeros((4 * tall, part.shape[2]), F32)
    t = 0
    for dz in range(3):
        for dy in range(3):
            for dx in range(3):
                lhs = jnp.concatenate(
                    [pad[x + dx, z + dz, dy : dy + tall, :] for z in range(2) for x in range(2)],
                    axis=0,
                ).astype(BF)
                acc = acc + jnp.dot(
                    lhs, weight[t * width : (t + 1) * width, :], preferred_element_type=F32
                )
                t += 1
    for j in range(n_my):
        for zx in range(4):
            part[j, 2 * zx : 2 * zx + 2, :] = acc[zx * tall + 2 * j : zx * tall + 2 * j + 2, :]


def lift_join(
    slots, chans, cells, n_my, slot_at, tgt, result, coarse, up, level, octs, sel,
    out, joined, sig, faces, ext, stage, lifted,
):
    ext[slots] = jnp.zeros((chans, VOL), BF)
    conv = jnp.concatenate([result[j] for j in range(n_my)], axis=1)
    co = (conv + coarse[...]).astype(BF)
    cof = co.astype(F32)
    for q in range(cells):
        z, x, y = q // 4, q // 2 % 2, q % 2
        out[(z * 2 + y) * 2 + x : (z * 2 + y) * 2 + x + 1, :] = cof[q : q + 1]
    width = 8 * chans
    wide = jnp.dot(co, up[...], preferred_element_type=F32)
    for p in range(8):
        lifted[p * cells : (p + 1) * cells, :] = wide[:, p * width : (p + 1) * width]
    pick = (
        lax.broadcasted_iota(jnp.int32, (chans, width), 0)
        == lax.broadcasted_iota(jnp.int32, (chans, width), 1) % chans
    )
    oc = octs[...]

    def step(j, c):
        row = jnp.where(pick, lifted[pl.ds(tgt[j], 1), :], 0.0)
        hi = row.astype(BF)
        lo = (row - hi.astype(F32)).astype(BF)
        both = jnp.dot(jnp.concatenate([hi, lo], axis=0), oc, preferred_element_type=F32)
        f = (level[j].astype(F32) + (both[:chans] + both[chans:])).astype(BF)
        joined[j] = f
        s = silu(f.astype(F32)).astype(BF)
        ext[j] = s
        sig[j] = s
        return c

    lax.fori_loop(0, slots, step, 0, unroll=2)
    pack_faces(slot_at, ext, sel, faces, stage, chans)


def conv_faces(
    slots, chans, slot_at, nb, base, sig, halo, sel, masks, weight,
    level, sig2, faces, ext, ext2, stage,
):
    ext[0:slots] = sig[...]
    ext[slots] = jnp.zeros((chans, VOL), BF)
    ext2[slots] = jnp.zeros((chans, VOL), BF)
    unpack_faces(ext, halo, sel, stage, slots, chans)
    w = weight[...]

    def step(j, c):
        f = (base[j].astype(F32) + conv_slot(j, nb, ext, masks, w)).astype(BF)
        level[j] = f
        s = silu(f.astype(F32)).astype(BF)
        ext2[j] = s
        sig2[j] = s
        return c

    lax.fori_loop(0, slots, step, 0, unroll=2)
    pack_faces(slot_at, ext2, sel, faces, stage, chans)


def conv_last(
    slots, chans, counts, nb, base, sig, halo, sel, masks, weight, out, ext, stage
):
    ext[0:slots] = sig[...]
    ext[slots] = jnp.zeros((chans, VOL), BF)
    unpack_faces(ext, halo, sel, stage, slots, chans)
    w = weight[...]
    n = counts[0]

    def step(j, c):
        f = base[j].astype(F32) + conv_slot(j, nb, ext, masks, w)
        out[j] = jnp.where(j < n, f, 0.0).astype(BF)
        return c

    lax.fori_loop(0, slots, step, 0, unroll=2)


def halo_kernel(faces, halo, send, recv):
    n_mx, n_my = lax.axis_size("mx"), lax.axis_size("my")
    mx, my = lax.axis_index("mx"), lax.axis_index("my")
    peers = (
        (my > 0, mx, my - 1),
        (my < n_my - 1, mx, my + 1),
        (mx > 0, mx - 1, my),
        (mx < n_mx - 1, mx + 1, my),
    )
    barrier = pltpu.get_barrier_semaphore()
    for has, a, b in peers:
        @pl.when(has)
        def _():
            pl.semaphore_signal(barrier, inc=1, device_id=(a, b), device_id_type=MESH)
    pl.semaphore_wait(barrier, sum(jnp.where(has, 1, 0) for has, _, _ in peers))

    def copy(f):
        has, a, b = peers[f]
        return pltpu.make_async_remote_copy(
            src_ref=faces.at[f], dst_ref=halo.at[f], send_sem=send.at[f], recv_sem=recv.at[f],
            device_id=(a, b), device_id_type=MESH,
        )

    for f in range(4):
        @pl.when(peers[f][0])
        def _():
            copy(f).start()

        @pl.when(jnp.logical_not(peers[f ^ 1][0]))
        def _():
            halo[f] = jnp.zeros_like(halo[f])
    for f in range(4):
        @pl.when(peers[f][0])
        def _():
            copy(f).wait_send()

        @pl.when(peers[f ^ 1][0])
        def _():
            copy(f).wait_recv()


def gather_kernel(coarse, stats, window, everyone, send, recv, wsend, wrecv):
    n_mx, n_my = lax.axis_size("mx"), lax.axis_size("my")
    mx, my = lax.axis_index("mx"), lax.axis_index("my")
    n = n_mx * n_my
    me = mx * n_my + my
    barrier = pltpu.get_barrier_semaphore()

    def greet(d, c):
        t = lax.rem(me + d, n)
        pl.semaphore_signal(
            barrier, inc=1, device_id=(t // n_my, lax.rem(t, n_my)), device_id_type=MESH
        )
        return c

    lax.fori_loop(1, n, greet, 0)
    pl.semaphore_wait(barrier, n - 1)

    def stat_copy(d):
        t = lax.rem(me + d, n)
        return pltpu.make_async_remote_copy(
            src_ref=stats, dst_ref=everyone.at[me], send_sem=send.at[d], recv_sem=recv.at[d],
            device_id=(t // n_my, lax.rem(t, n_my)), device_id_type=MESH,
        )

    def go(d, c):
        stat_copy(d).start()
        return c

    def wait(d, c):
        stat_copy(d).wait()
        return c

    def win_copy(kind, d):
        t = lax.rem(my + d, n_my)
        if kind == 0:
            src, dst, a = coarse, window.at[my, pl.ds(1, 2)], mx
        elif kind == 1:
            src, dst, a = coarse.at[pl.ds(0, 1)], window.at[my, pl.ds(3, 1)], mx - 1
        else:
            src, dst, a = coarse.at[pl.ds(1, 1)], window.at[my, pl.ds(0, 1)], mx + 1
        return pltpu.make_async_remote_copy(
            src_ref=src, dst_ref=dst, send_sem=wsend.at[kind, d], recv_sem=wrecv.at[kind, d],
            device_id=(a, t), device_id_type=MESH,
        )

    low, high = mx > 0, mx < n_mx - 1
    for d in range(n_my):
        if d:
            win_copy(0, d).start()

        @pl.when(low)
        def _():
            win_copy(1, d).start()

        @pl.when(high)
        def _():
            win_copy(2, d).start()
    lax.fori_loop(1, n, go, 0)
    window[my, 1:3] = coarse[...]
    everyone[me] = stats[...]

    @pl.when(jnp.logical_not(low))
    def _():
        for j in range(n_my):
            window[j, 0] = jnp.zeros_like(window[j, 0])

    @pl.when(jnp.logical_not(high))
    def _():
        for j in range(n_my):
            window[j, 3] = jnp.zeros_like(window[j, 3])

    for d in range(n_my):
        if d:
            win_copy(0, d).wait()

        @pl.when(low)
        def _():
            win_copy(1, d).wait_send()
            win_copy(2, d).wait_recv()

        @pl.when(high)
        def _():
            win_copy(2, d).wait_send()
            win_copy(1, d).wait_recv()
    lax.fori_loop(1, n, wait, 0)


def result_kernel(part, result, send, recv):
    n_my = lax.axis_size("my")
    mx, my = lax.axis_index("mx"), lax.axis_index("my")
    barrier = pltpu.get_barrier_semaphore()
    for d in range(1, n_my):
        pl.semaphore_signal(
            barrier, inc=1, device_id=(mx, lax.rem(my + d, n_my)), device_id_type=MESH
        )
    pl.semaphore_wait(barrier, n_my - 1)
    copies = []
    for d in range(1, n_my):
        t = lax.rem(my + d, n_my)
        copies.append(
            pltpu.make_async_remote_copy(
                src_ref=part.at[t], dst_ref=result.at[my], send_sem=send.at[d],
                recv_sem=recv.at[d], device_id=(mx, t), device_id_type=MESH,
            )
        )
    for c in copies:
        c.start()
    result[my] = part[my]
    for c in copies:
        c.wait()


def call(fn, out, scratch, n_smem, n_vmem, cid=None):
    params = {} if cid is None else {"collective_id": cid, "has_side_effects": True}
    return pl.pallas_call(
        fn,
        out_shape=out,
        in_specs=[SM] * n_smem + [VM] * n_vmem,
        out_specs=jax.tree.map(lambda _: VM, out),
        scratch_shapes=scratch,
        compiler_params=pltpu.CompilerParams(**params),
    )


def local(
    features, coords, counts, neighbours, fine_weights, down_weight, up_weight, norm_gain,
    norm_bias, coarse_weight,
):
    slots, chans, _ = features.shape
    n_mx, n_my = lax.axis_size("mx"), lax.axis_size("my")
    major, minor = lax.axis_index("mx"), lax.axis_index("my")
    cells = (RZ // 2) * (RY // 2) * (RX // 2)
    width = down_weight.shape[1]
    masks, sel, pool, spread, octs = constants(chans)
    first_slot = (major * n_my + minor) * slots
    live = jnp.arange(slots, dtype=jnp.int32) < counts[0]
    lz = coords[0] - major * RZ
    ly = coords[1] - minor * RY
    lx = coords[2]
    lin = jnp.where(live, (lz * RY + ly) * RX + lx, -1)
    hit = lin[None, :] == jnp.arange(RZ * RY * RX, dtype=jnp.int32)[:, None]
    ids = jnp.arange(slots, dtype=jnp.int32)
    slot_at = slots + jnp.sum(jnp.where(hit, ids - slots, 0), axis=1)
    here = neighbours - first_slot
    spots = jnp.stack([lz * RX + lx] * 4 + [ly * RX + lx] * 2)
    spots = spots + jnp.maximum(jnp.arange(6, dtype=jnp.int32) - 2, 0)[:, None] * NPOS + slots + 1
    nb = jnp.where(here < 0, spots, jnp.where(here >= slots, spots, here))
    nb = jnp.where(neighbours < 0, slots, nb)
    q = (lz // 2 * 2 + lx // 2) * 2 + ly // 2
    p = lz % 2 * 4 + ly % 2 * 2 + lx % 2
    tgt = jnp.where(live, p * cells + q, 0)

    sds = jax.ShapeDtypeStruct
    block = sds((slots, chans, VOL), BF)
    face = sds((4, NPOS // 2 * chans, 2 * SQ), BF)
    ext_rows = slots + 1 + 4 * NPOS
    ext = pltpu.VMEM((ext_rows, chans, VOL), BF)
    ext_small = pltpu.VMEM((slots + 1, chans, VOL), BF)
    stage = pltpu.VMEM((NPOS // 2 * chans, 2 * VOL), BF)
    dma = pltpu.SemaphoreType.DMA

    def exchange(faces, cid):
        return call(halo_kernel, face, [dma((4,)), dma((4,))], 0, 1, cid)(faces)

    sig, faces = call(
        functools.partial(first_faces, slots, chans), (block, face), [ext_small, stage], 1, 2
    )(slot_at, features, sel)
    halo = exchange(faces, 0)
    level, coarse, stats = call(
        functools.partial(conv_pool, slots, chans, cells),
        (block, sds((cells, width), F32), sds((2, width), F32)),
        [ext, stage, pltpu.VMEM((slots + 1, 8, chans), F32),
         pltpu.VMEM((8 * cells * 8, chans), F32)],
        2, 9,
    )(slot_at, nb, features, sig, halo, sel, masks, fine_weights[0], pool, spread, down_weight)
    n = n_mx * n_my
    window, everyone = call(
        gather_kernel,
        (sds((n_my, 4, 2, 2, width), F32), sds((n, 2, width), F32)),
        [dma((n,)), dma((n,)), dma((3, n_my)), dma((3, n_my))],
        0, 2, 1,
    )(coarse.reshape(2, 2, 2, width), stats)
    entries = float(cells * (width // GROUPS) * n)
    part = call(
        functools.partial(coarse_part, n_my, entries),
        sds((n_my, cells, coarse_weight.shape[1]), F32),
        [pltpu.VMEM((4, 4, -(-(2 * n_my + 2) // 8) * 8, width), F32)],
        0, 5,
    )(everyone, window, norm_gain[None, :], norm_bias[None, :], coarse_weight)
    result = call(
        result_kernel, sds(part.shape, F32), [dma((n_my,)), dma((n_my,))], 0, 1, 2
    )(part)
    out, joined, sig, faces = call(
        functools.partial(lift_join, slots, chans, cells, n_my),
        (sds((cells, width), F32), block, block, face),
        [ext_small, stage, pltpu.VMEM((8 * cells, 8 * chans), F32)],
        2, 6,
    )(slot_at, tgt, result, coarse, up_weight, level, octs, sel)
    halo = exchange(faces, 3)
    level, sig, faces = call(
        functools.partial(conv_faces, slots, chans),
        (block, block, face),
        [ext, ext_small, stage],
        2, 6,
    )(slot_at, nb, joined, sig, halo, sel, masks, fine_weights[1])
    halo = exchange(faces, 4)
    fine = call(
        functools.partial(conv_last, slots, chans), block, [ext, stage], 2, 6
    )(counts, nb, level, sig, halo, sel, masks, fine_weights[2])
    return fine, out.astype(BF).reshape(RZ // 2, RY // 2, RX // 2, width)


def solution(mesh):
    in_specs = (
        P(("mx", "my"), None, None),
        P(None, ("mx", "my")),
        P(("mx", "my")),
        P(None, ("mx", "my")),
        P(),
        P(),
        P(),
        P(),
        P(),
        P(None, "my"),
    )
    out_specs = (P(("mx", "my"), None, None), P("mx", "my", None, None))
    return jax.shard_map(local, mesh=mesh, in_specs=in_specs, out_specs=out_specs, check_vma=False)
```

```python
import functools

import jax
import jax.numpy as jnp
import numpy as np
from jax import lax
from jax.experimental import pallas as pl
from jax.experimental.pallas import tpu as pltpu
from jax.sharding import PartitionSpec as P

GROUPS = 32
SIDE = 8
RZ = 4
RY = 4
RX = 4
VOL = SIDE**3
SQ = SIDE * SIDE
NPOS = 16
norm_eps = 1e-05
MESH = pl.DeviceIdType.MESH
BF = jnp.bfloat16
F32 = jnp.float32
VM = pl.BlockSpec(memory_space=pltpu.VMEM)
SM = pl.BlockSpec(memory_space=pltpu.SMEM)


def constants(chans):
    v = np.arange(VOL)
    x, y, z = v % SIDE, v // SIDE % SIDE, v // SQ
    last = SIDE - 1
    masks = np.stack([x < last, x > 0, y < last, y > 0, z < last, z > 0])
    masks = np.broadcast_to(masks[:, None, :], (6, chans, VOL)).astype(np.float32)
    where = (y == 0, y == last, z == 0, z == last)
    spot = (z * SIDE + x, z * SIDE + x, y * SIDE + x, y * SIDE + x)
    sel = np.zeros((4, 2 * VOL, 2 * SQ), np.float32)
    for f in range(4):
        hit = np.nonzero(where[f])[0]
        sel[f, hit, spot[f][hit]] = 1
        sel[f, VOL + hit, SQ + spot[f][hit]] = 1
    half = SIDE // 2
    octant = z // half * 4 + y // half * 2 + x // half
    pool = (octant[None, :] == np.arange(8)[:, None]) / float(half**3)
    lanes = np.arange(8 * chans)
    spread = (np.arange(chans)[:, None] == lanes[None, :] % chans).astype(np.float32)
    octs = (lanes[:, None] // chans == octant[None, :]).astype(np.float32)
    as_bf = lambda a: jnp.asarray(a, BF)
    return as_bf(masks), as_bf(sel), as_bf(pool), as_bf(spread), as_bf(octs)


def silu(x):
    return x * jax.nn.sigmoid(x)


def face_slot(slot_at, face, k):
    a, b = k // 4, k % 4
    if face == 0:
        p = (a * RY + 0) * RX + b
    elif face == 1:
        p = (a * RY + RY - 1) * RX + b
    elif face == 2:
        p = (0 * RY + a) * RX + b
    else:
        p = ((RZ - 1) * RY + a) * RX + b
    return slot_at[p]


SHIFTS = ((-1, 7), (1, -7), (-8, 56), (8, -56), (-64, 448), (64, -448))


def tap(d, own, near, masks):
    a, b = SHIFTS[d]
    return jnp.where(masks[d] > 0.5, pltpu.roll(own, a % VOL, 1), pltpu.roll(near, b % VOL, 1))


def level_kernel(
    slots, chans, cells,
    slot_at, coords, counts, neighbours,
    feat, fine_w, gain, bias, pool, spread,
    masks_h, sel_h, octs_h, down_h, up_h, weight_h,
    out, coarse_out,
    masks, sel, octs, down, up, weight,
    ext, ext2, acc, level, stage, faces, halo, pooled, rows, coarse, stats,
    window, everyone, pad, part, result, lifted, nb, tgt,
    load, fsend, frecv, ssend, srecv, wsend, wrecv, rsend, rrecv,
):
    n_mx, n_my = lax.axis_size("mx"), lax.axis_size("my")
    mx, my = lax.axis_index("mx"), lax.axis_index("my")
    n = n_mx * n_my
    me = mx * n_my + my
    width = 8 * chans
    wide_c = gain.shape[1]

    loads = [
        pltpu.make_async_copy(a, b, load.at[i])
        for i, (a, b) in enumerate(
            ((sel_h, sel), (masks_h, masks), (down_h, down), (weight_h, weight),
             (up_h, up), (octs_h, octs))
        )
    ]
    for c in loads:
        c.start()

    barrier = pltpu.get_barrier_semaphore()

    def where_is(d):
        t = lax.rem(me + d, n)
        return (t // n_my, lax.rem(t, n_my))

    def greet(d, c):
        pl.semaphore_signal(barrier, inc=1, device_id=where_is(d), device_id_type=MESH)
        return c

    lax.fori_loop(1, n, greet, 0)

    ext[slots] = jnp.zeros((chans, VOL), BF)
    ext2[slots] = jnp.zeros((chans, VOL), BF)
    first_slot = me * slots
    count = counts[0]

    def begin(j, c):
        s = silu(feat[j].astype(F32)).astype(BF)
        ext[j] = s
        z = coords[0, j] - mx * RZ
        y = coords[1, j] - my * RY
        x = coords[2, j]
        for d in range(6):
            g = neighbours[d, j]
            here = g - first_slot
            spot = jnp.clip((z if d < 4 else y) * RX + x, 0, NPOS - 1)
            far = slots + 1 + max(d - 2, 0) * NPOS + spot
            inside = (here >= 0) & (here < slots)
            nb[d, j] = jnp.where(g < 0, slots, jnp.where(inside, here, far))
        q = (z // 2 * 2 + x // 2) * 2 + y // 2
        p = z % 2 * 4 + y % 2 * 2 + x % 2
        tgt[j] = jnp.clip(jnp.where(j < count, p * cells + q, 0), 0, 8 * cells - 1)
        return c

    lax.fori_loop(0, slots, begin, 0, unroll=2)
    loads[0].wait()

    peers = (
        (my > 0, mx, my - 1),
        (my < n_my - 1, mx, my + 1),
        (mx > 0, mx - 1, my),
        (mx < n_mx - 1, mx + 1, my),
    )

    def face_copy(r, f):
        _, a, b = peers[f]
        return pltpu.make_async_remote_copy(
            src_ref=faces.at[r, f], dst_ref=halo.at[r, f], send_sem=fsend.at[r, f],
            recv_sem=frecv.at[r, f], device_id=(a, b), device_id_type=MESH,
        )

    def send_faces(r, src):
        for f in range(4):
            for k in range(NPOS):
                s = face_slot(slot_at, f, k)
                stage[
                    k // 2 * chans : (k // 2 + 1) * chans, k % 2 * VOL : (k % 2 + 1) * VOL
                ] = src[s]
            faces[r, f] = jnp.dot(stage[...], sel[f], preferred_element_type=F32).astype(BF)
            if r == 0 and f == 0:
                pl.semaphore_wait(barrier, n - 1)

            @pl.when(peers[f][0])
            def _():
                face_copy(r, f).start()

            @pl.when(jnp.logical_not(peers[f ^ 1][0]))
            def _():
                halo[r, f] = jnp.zeros_like(halo[r, f])

    def take_faces(r, dst):
        for f in range(4):
            @pl.when(peers[f][0])
            def _():
                face_copy(r, f).wait_send()

            @pl.when(peers[f ^ 1][0])
            def _():
                face_copy(r, f).wait_recv()

            stage[...] = lax.dot_general(
                halo[r, f], sel[f], (((1,), (1,)), ((), ())), preferred_element_type=F32
            ).astype(BF)
            for k in range(NPOS):
                dst[slots + 1 + f * NPOS + k] = stage[
                    k // 2 * chans : (k // 2 + 1) * chans, k % 2 * VOL : (k % 2 + 1) * VOL
                ]

    def conv(r, base, src, finish):
        w = fine_w[r]
        w_near, w_far = w[:, : 3 * chans], w[:, 3 * chans :]

        def near_pass(j, c):
            own = src[j]
            taps = [own] + [tap(d, own, src[nb[d, j]], masks) for d in (0, 1)]
            acc[j] = base[j].astype(F32) + jnp.dot(
                w_near, jnp.concatenate(taps, axis=0), preferred_element_type=F32
            )
            return c

        lax.fori_loop(0, slots, near_pass, 0, unroll=2)
        take_faces(r, src)

        def far_pass(j, c):
            own = src[j]
            taps = [tap(d, own, src[nb[d, j]], masks) for d in (2, 3, 4, 5)]
            finish(
                j,
                acc[j] + jnp.dot(
                    w_far, jnp.concatenate(taps, axis=0), preferred_element_type=F32
                ),
            )
            return c

        lax.fori_loop(0, slots, far_pass, 0, unroll=2)

    send_faces(0, ext)
    loads[1].wait()

    pooled[slots] = jnp.zeros((8, chans), F32)
    pm = pool[...]

    def first_done(j, value):
        f = value.astype(BF)
        level[j] = f
        pooled[j] = lax.dot_general(pm, f, (((1,), (1,)), ((), ())), preferred_element_type=F32)

    conv(0, feat, ext, first_done)
    for p in range(8):
        for q in range(cells):
            z = q // 4 * 2 + p // 4
            x = q // 2 % 2 * 2 + p % 2
            y = q % 2 * 2 + p // 2 % 2
            i = p * cells + q
            rows[i * 8 : (i + 1) * 8, :] = pooled[slot_at[(z * RY + y) * RX + x]]
    wide = jnp.dot(rows[...].astype(BF), spread[...], preferred_element_type=F32)
    m = 8 * cells
    oct_row = lax.broadcasted_iota(jnp.int32, (m * 8, width), 0) % 8
    oct_lane = lax.broadcasted_iota(jnp.int32, (m * 8, width), 1) // chans
    wide = jnp.where(oct_row == oct_lane, wide, 0.0)
    flat = jnp.sum(wide.reshape(m, 8, width), axis=1).astype(BF)
    loads[2].wait()
    ci = jnp.zeros((cells, wide_c), F32)
    for p in range(8):
        ci = ci + jnp.dot(
            flat[p * cells : (p + 1) * cells],
            down[p * width : (p + 1) * width, :],
            preferred_element_type=F32,
        )
    layer = cells // 2
    coarse[0] = ci[:layer]
    coarse[1] = ci[layer:]
    stats[0:1, :] = jnp.sum(ci, axis=0, keepdims=True)
    stats[1:2, :] = jnp.sum(ci * ci, axis=0, keepdims=True)

    def stat_copy(d):
        return pltpu.make_async_remote_copy(
            src_ref=stats, dst_ref=everyone.at[me], send_sem=ssend.at[d], recv_sem=srecv.at[d],
            device_id=where_is(d), device_id_type=MESH,
        )

    def stat_go(d, c):
        stat_copy(d).start()
        return c

    def stat_wait(d, c):
        stat_copy(d).wait()
        return c

    def win_copy(kind, d):
        t = lax.rem(my + d, n_my)
        if kind == 0:
            src, dst, a = coarse, window.at[my, pl.ds(1, 2)], mx
        elif kind == 1:
            src, dst, a = coarse.at[pl.ds(0, 1)], window.at[my, pl.ds(3, 1)], mx - 1
        else:
            src, dst, a = coarse.at[pl.ds(1, 1)], window.at[my, pl.ds(0, 1)], mx + 1
        return pltpu.make_async_remote_copy(
            src_ref=src, dst_ref=dst, send_sem=wsend.at[kind, d], recv_sem=wrecv.at[kind, d],
            device_id=(a, t), device_id_type=MESH,
        )

    lax.fori_loop(1, n, stat_go, 0)
    low, high = mx > 0, mx < n_mx - 1
    for d in range(n_my):
        if d:
            win_copy(0, d).start()

        @pl.when(low)
        def _():
            win_copy(1, d).start()

        @pl.when(high)
        def _():
            win_copy(2, d).start()
    window[my, 1:3] = coarse[...]
    everyone[me] = stats[...]

    @pl.when(jnp.logical_not(low))
    def _():
        for j in range(n_my):
            window[j, 0] = jnp.zeros_like(window[j, 0])

    @pl.when(jnp.logical_not(high))
    def _():
        for j in range(n_my):
            window[j, 3] = jnp.zeros_like(window[j, 3])

    pad[...] = jnp.zeros_like(pad)
    group = wide_c // GROUPS
    same = (
        lax.broadcasted_iota(jnp.int32, (wide_c, wide_c), 0) // group
        == lax.broadcasted_iota(jnp.int32, (wide_c, wide_c), 1) // group
    ).astype(F32)
    for c in loads[3:]:
        c.wait()
    for d in range(n_my):
        if d:
            win_copy(0, d).wait()

        @pl.when(low)
        def _():
            win_copy(1, d).wait_send()
            win_copy(2, d).wait_recv()

        @pl.when(high)
        def _():
            win_copy(2, d).wait_send()
            win_copy(1, d).wait_recv()
    lax.fori_loop(1, n, stat_wait, 0)

    total = float(cells * group) * n
    sums = jnp.sum(everyone[...], axis=0)
    sums = jnp.concatenate([sums, jnp.zeros((6, wide_c), F32)], axis=0)
    sums = jnp.dot(sums, same, precision=lax.Precision.HIGHEST, preferred_element_type=F32) / total
    mean = sums[0:1]
    std = jnp.sqrt(sums[1:2] - mean * mean + norm_eps)
    g = gain[...]
    b = bias[...]
    for zw in range(4):
        for j in range(n_my):
            value = silu((window[j, zw] - mean) / std * g + b)
            if zw == 0:
                value = jnp.where(low, value, 0.0)
            if zw == 3:
                value = jnp.where(high, value, 0.0)
            for x in range(2):
                pad[1 + x, zw, 1 + 2 * j : 3 + 2 * j, :] = value[2 * x : 2 * x + 2]
    tall = 2 * n_my
    sums = jnp.zeros((4 * tall, part.shape[2]), F32)
    t = 0
    for dz in range(3):
        for dy in range(3):
            for dx in range(3):
                lhs = jnp.concatenate(
                    [pad[x + dx, z + dz, dy : dy + tall, :] for z in range(2) for x in range(2)],
                    axis=0,
                ).astype(BF)
                sums = sums + lax.dot_general(
                    lhs, weight[:, t * wide_c : (t + 1) * wide_c], (((1,), (1,)), ((), ())),
                    preferred_element_type=F32,
                )
                t += 1
    for j in range(n_my):
        for zx in range(4):
            part[j, 2 * zx : 2 * zx + 2, :] = sums[zx * tall + 2 * j : zx * tall + 2 * j + 2, :]
    copies = []
    for d in range(1, n_my):
        to = lax.rem(my + d, n_my)
        copies.append(
            pltpu.make_async_remote_copy(
                src_ref=part.at[to], dst_ref=result.at[my], send_sem=rsend.at[d],
                recv_sem=rrecv.at[d], device_id=(mx, to), device_id_type=MESH,
            )
        )
    for c in copies:
        c.start()
    result[my] = part[my]
    for c in copies:
        c.wait()

    whole = jnp.concatenate([result[j] for j in range(n_my)], axis=1)
    co = (whole + jnp.concatenate([coarse[0], coarse[1]], axis=0)).astype(BF)
    cof = co.astype(F32)
    for q in range(cells):
        z, x, y = q // 4, q // 2 % 2, q % 2
        coarse_out[(z * 2 + y) * 2 + x : (z * 2 + y) * 2 + x + 1, :] = cof[q : q + 1]
    wide = jnp.dot(co, up[...], preferred_element_type=F32)
    for p in range(8):
        for q in range(cells):
            lifted[p * cells + q] = wide[q : q + 1, p * width : (p + 1) * width]
    pick = (
        lax.broadcasted_iota(jnp.int32, (chans, width), 0)
        == lax.broadcasted_iota(jnp.int32, (chans, width), 1) % chans
    )
    oc = octs[...]

    def join(j, c):
        row = jnp.where(pick, lifted[tgt[j]], 0.0)
        hi = row.astype(BF)
        lo = (row - hi.astype(F32)).astype(BF)
        both = jnp.dot(jnp.concatenate([hi, lo], axis=0), oc, preferred_element_type=F32)
        f = (level[j].astype(F32) + (both[:chans] + both[chans:])).astype(BF)
        level[j] = f
        ext[j] = silu(f.astype(F32)).astype(BF)
        return c

    lax.fori_loop(0, slots, join, 0, unroll=2)
    send_faces(1, ext)

    def second_done(j, value):
        f = value.astype(BF)
        level[j] = f
        ext2[j] = silu(f.astype(F32)).astype(BF)

    conv(1, level, ext, second_done)
    send_faces(2, ext2)

    def last_done(j, value):
        out[j] = jnp.where(j < count, value, 0.0).astype(BF)

    conv(2, level, ext2, last_done)


def local(
    features, coords, counts, neighbours, fine_weights, down_weight, up_weight, norm_gain,
    norm_bias, coarse_weight,
):
    slots, chans, _ = features.shape
    n_mx, n_my = lax.axis_size("mx"), lax.axis_size("my")
    major, minor = lax.axis_index("mx"), lax.axis_index("my")
    cells = (RZ // 2) * (RY // 2) * (RX // 2)
    width = down_weight.shape[1]
    masks, sel, pool, spread, octs = constants(chans)
    ids = jnp.arange(slots, dtype=jnp.int32)
    lin = ((coords[0] - major * RZ) * RY + coords[1] - minor * RY) * RX + coords[2]
    lin = jnp.where(ids < counts[0], lin, -1)
    hit = lin[None, :] == jnp.arange(RZ * RY * RX, dtype=jnp.int32)[:, None]
    slot_at = slots + jnp.sum(jnp.where(hit, ids - slots, 0), axis=1)
    n = n_mx * n_my
    sds = jax.ShapeDtypeStruct
    weight_t = coarse_weight.T
    held = [
        pltpu.VMEM(a.shape, a.dtype)
        for a in (masks, sel, octs, down_weight, up_weight, weight_t)
    ]
    ext = pltpu.VMEM((slots + 1 + 4 * NPOS, chans, VOL), BF)
    ext_small = pltpu.VMEM((slots, chans, VOL), BF)
    pairs = NPOS // 2 * chans
    dma = pltpu.SemaphoreType.DMA
    scratch = held + [
        ext, ext,
        pltpu.VMEM((slots, chans, VOL), F32),
        ext_small,
        pltpu.VMEM((pairs, 2 * VOL), BF),
        pltpu.VMEM((3, 4, pairs, 2 * SQ), BF),
        pltpu.VMEM((3, 4, pairs, 2 * SQ), BF),
        pltpu.VMEM((slots + 1, 8, chans), F32),
        pltpu.VMEM((8 * cells * 8, chans), F32),
        pltpu.VMEM((2, cells // 2, width), F32),
        pltpu.VMEM((2, width), F32),
        pltpu.VMEM((n_my, 4, cells // 2, width), F32),
        pltpu.VMEM((n, 2, width), F32),
        pltpu.VMEM((4, 4, -(-(2 * n_my + 2) // 8) * 8, width), F32),
        pltpu.VMEM((n_my, cells, coarse_weight.shape[1]), F32),
        pltpu.VMEM((n_my, cells, coarse_weight.shape[1]), F32),
        pltpu.VMEM((8 * cells, 1, 8 * chans), F32),
        pltpu.SMEM((6, slots), jnp.int32),
        pltpu.SMEM((slots,), jnp.int32),
        dma((6,)), dma((3, 4)), dma((3, 4)), dma((n,)), dma((n,)),
        dma((3, n_my)), dma((3, n_my)), dma((n_my,)), dma((n_my,)),
    ]
    fine, out = pl.pallas_call(
        functools.partial(level_kernel, slots, chans, cells),
        out_shape=(sds(features.shape, BF), sds((cells, width), F32)),
        in_specs=[SM] * 4 + [VM] * 6 + [pl.BlockSpec(memory_space=pl.ANY)] * 6,
        out_specs=(VM, VM),
        scratch_shapes=scratch,
        compiler_params=pltpu.CompilerParams(collective_id=0, has_side_effects=True),
    )(
        slot_at, coords, counts, neighbours, features, fine_weights, norm_gain[None, :],
        norm_bias[None, :], pool, spread, masks, sel, octs, down_weight, up_weight, weight_t,
    )
    return fine, out.astype(BF).reshape(RZ // 2, RY // 2, RX // 2, width)


def solution(mesh):
    in_specs = (
        P(("mx", "my"), None, None),
        P(None, ("mx", "my")),
        P(("mx", "my")),
        P(None, ("mx", "my")),
        P(),
        P(),
        P(),
        P(),
        P(),
        P(None, "my"),
    )
    out_specs = (P(("mx", "my"), None, None), P("mx", "my", None, None))
    return jax.shard_map(local, mesh=mesh, in_specs=in_specs, out_specs=out_specs, check_vma=False)
```

```python
import functools

import jax
import jax.numpy as jnp
import numpy as np
from jax import lax
from jax.experimental import pallas as pl
from jax.experimental.pallas import tpu as pltpu
from jax.sharding import PartitionSpec as P

GROUPS = 32
SIDE = 8
RZ = 4
RY = 4
RX = 4
VOL = SIDE**3
SQ = SIDE * SIDE
NPOS = 16
LANES = 2 * SQ
CHUNKS = VOL // LANES
norm_eps = 1e-05
MESH = pl.DeviceIdType.MESH
BF = jnp.bfloat16
F32 = jnp.float32
VM = pl.BlockSpec(memory_space=pltpu.VMEM)
SM = pl.BlockSpec(memory_space=pltpu.SMEM)


def constants(chans):
    v = np.arange(VOL)
    x, y, z = v % SIDE, v // SIDE % SIDE, v // SQ
    last = SIDE - 1
    lane = np.arange(LANES)
    near = [x < last, x > 0, y < last, y > 0]
    masks = [m[:LANES] for m in near] + [lane < SQ]
    masks += [lane // SIDE % SIDE == k for k in range(SIDE)]
    masks = np.broadcast_to(np.stack(masks)[:, None, :], (5 + SIDE, chans, LANES))
    half = SIDE // 2
    octant = z // half * 4 + y // half * 2 + x // half
    pool = (octant[None, :] == np.arange(8)[:, None]) / float(half**3)
    lanes = np.arange(8 * chans)
    spread = (np.arange(chans)[:, None] == lanes[None, :] % chans).astype(np.float32)
    octs = (lanes[:, None] // chans == octant[None, :]).astype(np.float32)
    as_bf = lambda a: jnp.asarray(np.asarray(a, np.float32), BF)
    return as_bf(masks), as_bf(pool), as_bf(spread), as_bf(octs)


def silu(x):
    return x * jax.nn.sigmoid(x)


def face_slot(slot_at, face, k):
    a, b = k // 4, k % 4
    if face == 0:
        p = (a * RY + 0) * RX + b
    elif face == 1:
        p = (a * RY + RY - 1) * RX + b
    elif face == 2:
        p = (0 * RY + a) * RX + b
    else:
        p = ((RZ - 1) * RY + a) * RX + b
    return slot_at[p]


def chunk(ref, row, i):
    return ref[row, :, i * LANES : (i + 1) * LANES]


def turn(value, shift):
    return pltpu.roll(value, shift % LANES, 1) if shift % LANES else value


def side_tap(src, j, row, shift, span, keep):
    parts = []
    for i in range(CHUNKS):
        own = turn(chunk(src, j, i), -shift)
        near = turn(chunk(src, row, i), shift * (span - 1))
        parts.append(jnp.where(keep, own, near))
    return jnp.concatenate(parts, axis=1)


def depth_taps(src, j, up, down, low):
    turned = [turn(chunk(src, down, CHUNKS - 1), SQ)]
    turned += [turn(chunk(src, j, i), SQ) for i in range(CHUNKS)]
    turned += [turn(chunk(src, up, 0), SQ)]
    plus = [jnp.where(low, turned[i + 1], turned[i + 2]) for i in range(CHUNKS)]
    minus = [jnp.where(low, turned[i], turned[i + 1]) for i in range(CHUNKS)]
    return jnp.concatenate(plus, axis=1), jnp.concatenate(minus, axis=1)


def level_kernel(
    slots, chans, cells,
    slot_at, coords, counts, neighbours,
    feat, fine_w, gain, bias, pool, spread, masks,
    octs_h, down_h, up_h, weight_h,
    out, coarse_out,
    octs, down, up, weight,
    ext, ext2, acc, level, faces, halo, pooled, rows, coarse, stats,
    window, everyone, pad, part, result, lifted, nb, tgt,
    load, fsend, frecv, ssend, srecv, wsend, wrecv, rsend, rrecv,
):
    n_mx, n_my = lax.axis_size("mx"), lax.axis_size("my")
    mx, my = lax.axis_index("mx"), lax.axis_index("my")
    n = n_mx * n_my
    me = mx * n_my + my
    width = 8 * chans
    wide_c = gain.shape[1]

    loads = [
        pltpu.make_async_copy(a, b, load.at[i])
        for i, (a, b) in enumerate(
            ((down_h, down), (weight_h, weight),
             (up_h, up), (octs_h, octs))
        )
    ]
    for c in loads:
        c.start()

    barrier = pltpu.get_barrier_semaphore()

    def where_is(d):
        t = lax.rem(me + d, n)
        return (t // n_my, lax.rem(t, n_my))

    def greet(d, c):
        pl.semaphore_signal(barrier, inc=1, device_id=where_is(d), device_id_type=MESH)
        return c

    lax.fori_loop(1, n, greet, 0)

    ext[slots] = jnp.zeros((chans, VOL), BF)
    ext2[slots] = jnp.zeros((chans, VOL), BF)
    first_slot = me * slots
    count = counts[0]

    def begin(j, c):
        s = silu(feat[j].astype(F32)).astype(BF)
        ext[j] = s
        z = coords[0, j] - mx * RZ
        y = coords[1, j] - my * RY
        x = coords[2, j]
        for d in range(6):
            g = neighbours[d, j]
            here = g - first_slot
            spot = jnp.clip((z if d < 4 else y) * RX + x, 0, NPOS - 1)
            far = slots + 1 + max(d - 2, 0) * NPOS + spot
            inside = (here >= 0) & (here < slots)
            nb[d, j] = jnp.where(g < 0, slots, jnp.where(inside, here, far))
        q = (z // 2 * 2 + x // 2) * 2 + y // 2
        p = z % 2 * 4 + y % 2 * 2 + x % 2
        tgt[j] = jnp.clip(jnp.where(j < count, p * cells + q, 0), 0, 8 * cells - 1)
        return c

    lax.fori_loop(0, slots, begin, 0, unroll=2)
    keep = [masks[i] > 0.5 for i in range(5)]
    low_half = keep[4]

    peers = (
        (my > 0, mx, my - 1),
        (my < n_my - 1, mx, my + 1),
        (mx > 0, mx - 1, my),
        (mx < n_mx - 1, mx + 1, my),
    )

    def face_copy(r, f):
        _, a, b = peers[f]
        return pltpu.make_async_remote_copy(
            src_ref=faces.at[r, f], dst_ref=halo.at[r, f], send_sem=fsend.at[r, f],
            recv_sem=frecv.at[r, f], device_id=(a, b), device_id_type=MESH,
        )

    def send_faces(r, src):
        for f in range(4):
            rows_of = [face_slot(slot_at, f, k) for k in range(NPOS)]
            if f < 2:
                for g in range(2):
                    for i in range(CHUNKS):
                        mixed = None
                        for k in range(SIDE):
                            v = chunk(src, rows_of[g * SIDE + k], i)
                            v = turn(v, SIDE * k - f * (SQ - SIDE))
                            mixed = v if k == 0 else jnp.where(masks[5 + k] > 0.5, v, mixed)
                        faces[r, f, g * CHUNKS + i] = mixed
            else:
                i = 0 if f == 2 else CHUNKS - 1
                for k in range(NPOS // 2):
                    a, b = chunk(src, rows_of[2 * k], i), chunk(src, rows_of[2 * k + 1], i)
                    if f == 2:
                        b = turn(b, SQ)
                    else:
                        a = turn(a, SQ)
                    faces[r, f, k] = jnp.where(low_half, a, b)
            if r == 0 and f == 0:
                pl.semaphore_wait(barrier, n - 1)

            @pl.when(peers[f][0])
            def _():
                face_copy(r, f).start()

            @pl.when(jnp.logical_not(peers[f ^ 1][0]))
            def _():
                halo[r, f] = jnp.zeros_like(halo[r, f])

    def take_faces(r, dst):
        for f in range(4):
            @pl.when(peers[f][0])
            def _():
                face_copy(r, f).wait_send()

            @pl.when(peers[f ^ 1][0])
            def _():
                face_copy(r, f).wait_recv()

            for k in range(NPOS):
                row = slots + 1 + f * NPOS + k
                if f < 2:
                    for i in range(CHUNKS):
                        v = halo[r, f, k // SIDE * CHUNKS + i]
                        v = turn(v, f * (SQ - SIDE) - SIDE * (k % SIDE))
                        dst[row, :, i * LANES : (i + 1) * LANES] = v
                else:
                    i = 0 if f == 2 else CHUNKS - 1
                    v = halo[r, f, k // 2]
                    if k % 2 != f - 2:
                        v = turn(v, SQ)
                    dst[row, :, i * LANES : (i + 1) * LANES] = v

    def conv(r, base, src, finish):
        w = fine_w[r]
        w_near, w_far = w[:, : 3 * chans], w[:, 3 * chans :]

        def near_pass(j, c):
            taps = [
                src[j],
                side_tap(src, j, nb[0, j], 1, SIDE, keep[0]),
                side_tap(src, j, nb[1, j], -1, SIDE, keep[1]),
            ]
            acc[j] = base[j].astype(F32) + jnp.dot(
                w_near, jnp.concatenate(taps, axis=0), preferred_element_type=F32
            )
            return c

        lax.fori_loop(0, slots, near_pass, 0, unroll=2)
        take_faces(r, src)

        def far_pass(j, c):
            taps = [
                side_tap(src, j, nb[2, j], SIDE, SIDE, keep[2]),
                side_tap(src, j, nb[3, j], -SIDE, SIDE, keep[3]),
                *depth_taps(src, j, nb[4, j], nb[5, j], low_half),
            ]
            finish(
                j,
                acc[j] + jnp.dot(
                    w_far, jnp.concatenate(taps, axis=0), preferred_element_type=F32
                ),
            )
            return c

        lax.fori_loop(0, slots, far_pass, 0, unroll=2)

    send_faces(0, ext)

    pooled[slots] = jnp.zeros((8, chans), F32)
    pm = pool[...]

    def first_done(j, value):
        f = value.astype(BF)
        level[j] = f
        pooled[j] = lax.dot_general(pm, f, (((1,), (1,)), ((), ())), preferred_element_type=F32)

    conv(0, feat, ext, first_done)
    for p in range(8):
        for q in range(cells):
            z = q // 4 * 2 + p // 4
            x = q // 2 % 2 * 2 + p % 2
            y = q % 2 * 2 + p // 2 % 2
            i = p * cells + q
            rows[i * 8 : (i + 1) * 8, :] = pooled[slot_at[(z * RY + y) * RX + x]]
    wide = jnp.dot(rows[...].astype(BF), spread[...], preferred_element_type=F32)
    m = 8 * cells
    oct_row = lax.broadcasted_iota(jnp.int32, (m * 8, width), 0) % 8
    oct_lane = lax.broadcasted_iota(jnp.int32, (m * 8, width), 1) // chans
    wide = jnp.where(oct_row == oct_lane, wide, 0.0)
    flat = jnp.sum(wide.reshape(m, 8, width), axis=1).astype(BF)
    loads[0].wait()
    ci = jnp.zeros((cells, wide_c), F32)
    for p in range(8):
        ci = ci + jnp.dot(
            flat[p * cells : (p + 1) * cells],
            down[p * width : (p + 1) * width, :],
            preferred_element_type=F32,
        )
    layer = cells // 2
    coarse[0] = ci[:layer]
    coarse[1] = ci[layer:]
    stats[0:1, :] = jnp.sum(ci, axis=0, keepdims=True)
    stats[1:2, :] = jnp.sum(ci * ci, axis=0, keepdims=True)

    def stat_copy(d):
        return pltpu.make_async_remote_copy(
            src_ref=stats, dst_ref=everyone.at[me], send_sem=ssend.at[d], recv_sem=srecv.at[d],
            device_id=where_is(d), device_id_type=MESH,
        )

    def stat_go(d, c):
        stat_copy(d).start()
        return c

    def stat_wait(d, c):
        stat_copy(d).wait()
        return c

    def win_copy(kind, d):
        t = lax.rem(my + d, n_my)
        if kind == 0:
            src, dst, a = coarse, window.at[my, pl.ds(1, 2)], mx
        elif kind == 1:
            src, dst, a = coarse.at[pl.ds(0, 1)], window.at[my, pl.ds(3, 1)], mx - 1
        else:
            src, dst, a = coarse.at[pl.ds(1, 1)], window.at[my, pl.ds(0, 1)], mx + 1
        return pltpu.make_async_remote_copy(
            src_ref=src, dst_ref=dst, send_sem=wsend.at[kind, d], recv_sem=wrecv.at[kind, d],
            device_id=(a, t), device_id_type=MESH,
        )

    lax.fori_loop(1, n, stat_go, 0)
    low, high = mx > 0, mx < n_mx - 1
    for d in range(n_my):
        if d:
            win_copy(0, d).start()

        @pl.when(low)
        def _():
            win_copy(1, d).start()

        @pl.when(high)
        def _():
            win_copy(2, d).start()
    window[my, 1:3] = coarse[...]
    everyone[me] = stats[...]

    @pl.when(jnp.logical_not(low))
    def _():
        for j in range(n_my):
            window[j, 0] = jnp.zeros_like(window[j, 0])

    @pl.when(jnp.logical_not(high))
    def _():
        for j in range(n_my):
            window[j, 3] = jnp.zeros_like(window[j, 3])

    pad[...] = jnp.zeros_like(pad)
    group = wide_c // GROUPS
    same = (
        lax.broadcasted_iota(jnp.int32, (wide_c, wide_c), 0) // group
        == lax.broadcasted_iota(jnp.int32, (wide_c, wide_c), 1) // group
    ).astype(F32)
    for c in loads[1:]:
        c.wait()
    for d in range(n_my):
        if d:
            win_copy(0, d).wait()

        @pl.when(low)
        def _():
            win_copy(1, d).wait_send()
            win_copy(2, d).wait_recv()

        @pl.when(high)
        def _():
            win_copy(2, d).wait_send()
            win_copy(1, d).wait_recv()
    lax.fori_loop(1, n, stat_wait, 0)

    total = float(cells * group) * n
    sums = jnp.sum(everyone[...], axis=0)
    sums = jnp.concatenate([sums, jnp.zeros((6, wide_c), F32)], axis=0)
    sums = jnp.dot(sums, same, precision=lax.Precision.HIGHEST, preferred_element_type=F32) / total
    mean = sums[0:1]
    std = jnp.sqrt(sums[1:2] - mean * mean + norm_eps)
    g = gain[...]
    b = bias[...]
    for zw in range(4):
        for j in range(n_my):
            value = silu((window[j, zw] - mean) / std * g + b)
            if zw == 0:
                value = jnp.where(low, value, 0.0)
            if zw == 3:
                value = jnp.where(high, value, 0.0)
            for x in range(2):
                pad[1 + x, zw, 1 + 2 * j : 3 + 2 * j, :] = value[2 * x : 2 * x + 2]
    tall = 2 * n_my
    sums = jnp.zeros((4 * tall, part.shape[2]), F32)
    t = 0
    for dz in range(3):
        for dy in range(3):
            for dx in range(3):
                lhs = jnp.concatenate(
                    [pad[x + dx, z + dz, dy : dy + tall, :] for z in range(2) for x in range(2)],
                    axis=0,
                ).astype(BF)
                sums = sums + lax.dot_general(
                    lhs, weight[:, t * wide_c : (t + 1) * wide_c], (((1,), (1,)), ((), ())),
                    preferred_element_type=F32,
                )
                t += 1
    for j in range(n_my):
        for zx in range(4):
            part[j, 2 * zx : 2 * zx + 2, :] = sums[zx * tall + 2 * j : zx * tall + 2 * j + 2, :]
    copies = []
    for d in range(1, n_my):
        to = lax.rem(my + d, n_my)
        copies.append(
            pltpu.make_async_remote_copy(
                src_ref=part.at[to], dst_ref=result.at[my], send_sem=rsend.at[d],
                recv_sem=rrecv.at[d], device_id=(mx, to), device_id_type=MESH,
            )
        )
    for c in copies:
        c.start()
    result[my] = part[my]
    for c in copies:
        c.wait()

    whole = jnp.concatenate([result[j] for j in range(n_my)], axis=1)
    co = (whole + jnp.concatenate([coarse[0], coarse[1]], axis=0)).astype(BF)
    cof = co.astype(F32)
    for z in range(2):
        for y in range(2):
            q = z * 4 + y
            pair = jnp.concatenate([cof[q : q + 1], cof[q + 2 : q + 3]], axis=0)
            coarse_out[z, y] = pair.astype(BF)
    wide = jnp.dot(co, up[...], preferred_element_type=F32)
    for p in range(8):
        for q in range(cells):
            lifted[p * cells + q] = wide[q : q + 1, p * width : (p + 1) * width]
    pick = (
        lax.broadcasted_iota(jnp.int32, (chans, width), 0)
        == lax.broadcasted_iota(jnp.int32, (chans, width), 1) % chans
    )
    oc = octs[...]

    def join(j, c):
        row = jnp.where(pick, lifted[tgt[j]], 0.0)
        hi = row.astype(BF)
        lo = (row - hi.astype(F32)).astype(BF)
        both = jnp.dot(jnp.concatenate([hi, lo], axis=0), oc, preferred_element_type=F32)
        f = (level[j].astype(F32) + (both[:chans] + both[chans:])).astype(BF)
        level[j] = f
        ext[j] = silu(f.astype(F32)).astype(BF)
        return c

    lax.fori_loop(0, slots, join, 0, unroll=2)
    send_faces(1, ext)

    def second_done(j, value):
        f = value.astype(BF)
        level[j] = f
        ext2[j] = silu(f.astype(F32)).astype(BF)

    conv(1, level, ext, second_done)
    send_faces(2, ext2)

    def last_done(j, value):
        out[j] = value.astype(BF)

    conv(2, level, ext2, last_done)


def local(
    features, coords, counts, neighbours, fine_weights, down_weight, up_weight, norm_gain,
    norm_bias, coarse_weight,
):
    slots, chans, _ = features.shape
    n_mx, n_my = lax.axis_size("mx"), lax.axis_size("my")
    major, minor = lax.axis_index("mx"), lax.axis_index("my")
    cells = (RZ // 2) * (RY // 2) * (RX // 2)
    width = down_weight.shape[1]
    masks, pool, spread, octs = constants(chans)
    ids = jnp.arange(slots, dtype=jnp.int32)
    lin = ((coords[0] - major * RZ) * RY + coords[1] - minor * RY) * RX + coords[2]
    lin = jnp.where(ids < counts[0], lin, -1)
    hit = lin[None, :] == jnp.arange(RZ * RY * RX, dtype=jnp.int32)[:, None]
    slot_at = slots + jnp.sum(jnp.where(hit, ids - slots, 0), axis=1)
    n = n_mx * n_my
    sds = jax.ShapeDtypeStruct
    weight_t = coarse_weight.T
    held = [
        pltpu.VMEM(a.shape, a.dtype)
        for a in (octs, down_weight, up_weight, weight_t)
    ]
    ext = pltpu.VMEM((slots + 1 + 4 * NPOS, chans, VOL), BF)
    ext_small = pltpu.VMEM((slots, chans, VOL), BF)
    dma = pltpu.SemaphoreType.DMA
    scratch = held + [
        ext, ext,
        pltpu.VMEM((slots, chans, VOL), F32),
        ext_small,
        pltpu.VMEM((3, 4, NPOS // 2, chans, LANES), BF),
        pltpu.VMEM((3, 4, NPOS // 2, chans, LANES), BF),
        pltpu.VMEM((slots + 1, 8, chans), F32),
        pltpu.VMEM((8 * cells * 8, chans), F32),
        pltpu.VMEM((2, cells // 2, width), F32),
        pltpu.VMEM((2, width), F32),
        pltpu.VMEM((n_my, 4, cells // 2, width), F32),
        pltpu.VMEM((n, 2, width), F32),
        pltpu.VMEM((4, 4, -(-(2 * n_my + 2) // 8) * 8, width), F32),
        pltpu.VMEM((n_my, cells, coarse_weight.shape[1]), F32),
        pltpu.VMEM((n_my, cells, coarse_weight.shape[1]), F32),
        pltpu.VMEM((8 * cells, 1, 8 * chans), F32),
        pltpu.SMEM((6, slots), jnp.int32),
        pltpu.SMEM((slots,), jnp.int32),
        dma((4,)), dma((3, 4)), dma((3, 4)), dma((n,)), dma((n,)),
        dma((3, n_my)), dma((3, n_my)), dma((n_my,)), dma((n_my,)),
    ]
    fine, out = pl.pallas_call(
        functools.partial(level_kernel, slots, chans, cells),
        out_shape=(sds(features.shape, BF), sds((RZ // 2, RY // 2, RX // 2, width), BF)),
        in_specs=[SM] * 4 + [VM] * 7 + [pl.BlockSpec(memory_space=pl.ANY)] * 4,
        out_specs=(VM, VM),
        scratch_shapes=scratch,
        compiler_params=pltpu.CompilerParams(collective_id=0, has_side_effects=True),
    )(
        slot_at, coords, counts, neighbours, features, fine_weights, norm_gain[None, :],
        norm_bias[None, :], pool, spread, masks, octs, down_weight, up_weight, weight_t,
    )
    fine = jnp.where((ids < counts[0])[:, None, None], fine, jnp.zeros_like(fine))
    return fine, out


def solution(mesh):
    in_specs = (
        P(("mx", "my"), None, None),
        P(None, ("mx", "my")),
        P(("mx", "my")),
        P(None, ("mx", "my")),
        P(),
        P(),
        P(),
        P(),
        P(),
        P(None, "my"),
    )
    out_specs = (P(("mx", "my"), None, None), P("mx", "my", None, None))
    return jax.shard_map(local, mesh=mesh, in_specs=in_specs, out_specs=out_specs, check_vma=False)
```

```python
import functools

import jax
import jax.numpy as jnp
import numpy as np
from jax import lax
from jax.experimental import pallas as pl
from jax.experimental.pallas import tpu as pltpu
from jax.sharding import PartitionSpec as P

GROUPS = 32
SIDE = 8
RZ = 4
RY = 4
RX = 4
VOL = SIDE**3
SQ = SIDE * SIDE
NPOS = 16
UNROLL = 8
LANES = 2 * SQ
CHUNKS = VOL // LANES
norm_eps = 1e-05
MESH = pl.DeviceIdType.MESH
BF = jnp.bfloat16
F32 = jnp.float32
VM = pl.BlockSpec(memory_space=pltpu.VMEM)
SM = pl.BlockSpec(memory_space=pltpu.SMEM)


def constants(chans):
    v = np.arange(VOL)
    x, y, z = v % SIDE, v // SIDE % SIDE, v // SQ
    last = SIDE - 1
    lane = np.arange(LANES)
    near = [x < last, x > 0, y < last, y > 0]
    masks = [m[:LANES] for m in near] + [lane < SQ]
    masks += [lane // SIDE % SIDE == k for k in range(SIDE)]
    masks = np.broadcast_to(np.stack(masks)[:, None, :], (5 + SIDE, chans, LANES))
    half = SIDE // 2
    octant = z // half * 4 + y // half * 2 + x // half
    pool = (octant[None, :] == np.arange(8)[:, None]) / float(half**3)
    lanes = np.arange(8 * chans)
    spread = (np.arange(chans)[:, None] == lanes[None, :] % chans).astype(np.float32)
    octs = (lanes[:, None] // chans == octant[None, :]).astype(np.float32)
    as_bf = lambda a: jnp.asarray(np.asarray(a, np.float32), BF)
    return as_bf(masks), as_bf(pool), as_bf(spread), as_bf(octs)


def silu(x):
    h = 0.5 * x
    return h * jnp.tanh(h) + h


def face_slot(slot_at, face, k):
    a, b = k // 4, k % 4
    if face == 0:
        p = (a * RY + 0) * RX + b
    elif face == 1:
        p = (a * RY + RY - 1) * RX + b
    elif face == 2:
        p = (0 * RY + a) * RX + b
    else:
        p = ((RZ - 1) * RY + a) * RX + b
    return slot_at[p]


def chunk(ref, row, i):
    return ref[row, :, i * LANES : (i + 1) * LANES]


def turn(value, shift):
    return pltpu.roll(value, shift % LANES, 1) if shift % LANES else value


def side_tap(src, j, row, shift, span, keep):
    parts = []
    for i in range(CHUNKS):
        own = turn(chunk(src, j, i), -shift)
        near = turn(chunk(src, row, i), shift * (span - 1))
        parts.append(jnp.where(keep, own, near))
    return jnp.concatenate(parts, axis=1)


def depth_taps(src, j, up, down, low):
    turned = [turn(chunk(src, down, CHUNKS - 1), SQ)]
    turned += [turn(chunk(src, j, i), SQ) for i in range(CHUNKS)]
    turned += [turn(chunk(src, up, 0), SQ)]
    plus = [jnp.where(low, turned[i + 1], turned[i + 2]) for i in range(CHUNKS)]
    minus = [jnp.where(low, turned[i], turned[i + 1]) for i in range(CHUNKS)]
    return jnp.concatenate(plus, axis=1), jnp.concatenate(minus, axis=1)


def level_kernel(
    slots, chans, cells,
    slot_at, coords, counts, neighbours,
    feat, fine_w, gain, bias, pool, spread, masks,
    octs_h, down_h, up_h, weight_h,
    out, coarse_out,
    octs, down, up, weight,
    ext, ext2, acc, level, faces, halo, pooled, rows, coarse, stats,
    window, everyone, pad, part, result, lifted, nb, tgt,
    load, fsend, frecv, ssend, srecv, wsend, wrecv, rsend, rrecv,
):
    n_mx, n_my = lax.axis_size("mx"), lax.axis_size("my")
    mx, my = lax.axis_index("mx"), lax.axis_index("my")
    n = n_mx * n_my
    me = mx * n_my + my
    width = 8 * chans
    wide_c = gain.shape[1]

    loads = [
        pltpu.make_async_copy(a, b, load.at[i])
        for i, (a, b) in enumerate(
            ((down_h, down), (weight_h, weight),
             (up_h, up), (octs_h, octs))
        )
    ]
    for c in loads:
        c.start()

    barrier = pltpu.get_barrier_semaphore()

    def where_is(d):
        t = lax.rem(me + d, n)
        return (t // n_my, lax.rem(t, n_my))

    def greet(d, c):
        pl.semaphore_signal(barrier, inc=1, device_id=where_is(d), device_id_type=MESH)
        return c

    lax.fori_loop(1, n, greet, 0)

    ext[slots] = jnp.zeros((chans, VOL), BF)
    ext2[slots] = jnp.zeros((chans, VOL), BF)
    first_slot = me * slots
    count = counts[0]

    def tables(j):
        z = coords[0, j] - mx * RZ
        y = coords[1, j] - my * RY
        x = coords[2, j]
        for d in range(6):
            g = neighbours[d, j]
            here = g - first_slot
            spot = jnp.clip((z if d < 4 else y) * RX + x, 0, NPOS - 1)
            far = slots + 1 + max(d - 2, 0) * NPOS + spot
            inside = (here >= 0) & (here < slots)
            nb[d, j] = jnp.where(g < 0, slots, jnp.where(inside, here, far))
        q = (z // 2 * 2 + x // 2) * 2 + y // 2
        p = z % 2 * 4 + y % 2 * 2 + x % 2
        tgt[j] = jnp.clip(jnp.where(j < count, p * cells + q, 0), 0, 8 * cells - 1)

    def begin(j, c):
        s = silu(feat[j].astype(F32)).astype(BF)
        ext[j] = s
        return c

    lax.fori_loop(0, slots, begin, 0, unroll=UNROLL)
    keep = [masks[i] > 0.5 for i in range(5)]
    low_half = keep[4]

    peers = (
        (my > 0, mx, my - 1),
        (my < n_my - 1, mx, my + 1),
        (mx > 0, mx - 1, my),
        (mx < n_mx - 1, mx + 1, my),
    )

    def face_copy(r, f):
        _, a, b = peers[f]
        return pltpu.make_async_remote_copy(
            src_ref=faces.at[r, f], dst_ref=halo.at[r, f], send_sem=fsend.at[r, f],
            recv_sem=frecv.at[r, f], device_id=(a, b), device_id_type=MESH,
        )

    def send_faces(r, src):
        for f in range(4):
            rows_of = [face_slot(slot_at, f, k) for k in range(NPOS)]
            if f < 2:
                for g in range(2):
                    for i in range(CHUNKS):
                        mixed = None
                        for k in range(SIDE):
                            v = chunk(src, rows_of[g * SIDE + k], i)
                            v = turn(v, SIDE * k - f * (SQ - SIDE))
                            mixed = v if k == 0 else jnp.where(masks[5 + k] > 0.5, v, mixed)
                        faces[r, f, g * CHUNKS + i] = mixed
            else:
                i = 0 if f == 2 else CHUNKS - 1
                for k in range(NPOS // 2):
                    a, b = chunk(src, rows_of[2 * k], i), chunk(src, rows_of[2 * k + 1], i)
                    if f == 2:
                        b = turn(b, SQ)
                    else:
                        a = turn(a, SQ)
                    faces[r, f, k] = jnp.where(low_half, a, b)
            if r == 0 and f == 0:
                pl.semaphore_wait(barrier, n - 1)

            @pl.when(peers[f][0])
            def _():
                face_copy(r, f).start()

            @pl.when(jnp.logical_not(peers[f ^ 1][0]))
            def _():
                halo[r, f] = jnp.zeros_like(halo[r, f])

    def take_faces(r, dst):
        for f in range(4):
            @pl.when(peers[f][0])
            def _():
                face_copy(r, f).wait_send()

            @pl.when(peers[f ^ 1][0])
            def _():
                face_copy(r, f).wait_recv()

            for k in range(NPOS):
                row = slots + 1 + f * NPOS + k
                if f < 2:
                    for i in range(CHUNKS):
                        v = halo[r, f, k // SIDE * CHUNKS + i]
                        v = turn(v, f * (SQ - SIDE) - SIDE * (k % SIDE))
                        dst[row, :, i * LANES : (i + 1) * LANES] = v
                else:
                    i = 0 if f == 2 else CHUNKS - 1
                    v = halo[r, f, k // 2]
                    if k % 2 != f - 2:
                        v = turn(v, SQ)
                    dst[row, :, i * LANES : (i + 1) * LANES] = v

    def conv(r, base, src, finish):
        w = fine_w[r]
        w_near, w_far = w[:, : 3 * chans], w[:, 3 * chans :]

        def near_pass(j, c):
            if r == 0:
                tables(j)
            taps = [
                src[j],
                side_tap(src, j, nb[0, j], 1, SIDE, keep[0]),
                side_tap(src, j, nb[1, j], -1, SIDE, keep[1]),
            ]
            acc[j] = base[j].astype(F32) + jnp.dot(
                w_near, jnp.concatenate(taps, axis=0), preferred_element_type=F32
            )
            return c

        lax.fori_loop(0, slots, near_pass, 0, unroll=UNROLL)
        take_faces(r, src)

        def far_pass(j, c):
            taps = [
                side_tap(src, j, nb[2, j], SIDE, SIDE, keep[2]),
                side_tap(src, j, nb[3, j], -SIDE, SIDE, keep[3]),
                *depth_taps(src, j, nb[4, j], nb[5, j], low_half),
            ]
            finish(
                j,
                acc[j] + jnp.dot(
                    w_far, jnp.concatenate(taps, axis=0), preferred_element_type=F32
                ),
            )
            return c

        lax.fori_loop(0, slots, far_pass, 0, unroll=UNROLL)

    send_faces(0, ext)

    pooled[slots] = jnp.zeros((8, chans), F32)
    pm = pool[...]

    def first_done(j, value):
        f = value.astype(BF)
        level[j] = f
        pooled[j] = lax.dot_general(pm, f, (((1,), (1,)), ((), ())), preferred_element_type=F32)

    conv(0, feat, ext, first_done)
    for p in range(8):
        for q in range(cells):
            z = q // 4 * 2 + p // 4
            x = q // 2 % 2 * 2 + p % 2
            y = q % 2 * 2 + p // 2 % 2
            i = p * cells + q
            rows[i * 8 : (i + 1) * 8, :] = pooled[slot_at[(z * RY + y) * RX + x]]
    wide = jnp.dot(rows[...].astype(BF), spread[...], preferred_element_type=F32)
    m = 8 * cells
    oct_row = lax.broadcasted_iota(jnp.int32, (m * 8, width), 0) % 8
    oct_lane = lax.broadcasted_iota(jnp.int32, (m * 8, width), 1) // chans
    wide = jnp.where(oct_row == oct_lane, wide, 0.0)
    flat = jnp.sum(wide.reshape(m, 8, width), axis=1).astype(BF)
    loads[0].wait()
    ci = jnp.zeros((cells, wide_c), F32)
    for p in range(8):
        ci = ci + jnp.dot(
            flat[p * cells : (p + 1) * cells],
            down[p * width : (p + 1) * width, :],
            preferred_element_type=F32,
        )
    layer = cells // 2
    coarse[0] = ci[:layer]
    coarse[1] = ci[layer:]
    stats[0:1, :] = jnp.sum(ci, axis=0, keepdims=True)
    stats[1:2, :] = jnp.sum(ci * ci, axis=0, keepdims=True)

    def stat_copy(d):
        return pltpu.make_async_remote_copy(
            src_ref=stats, dst_ref=everyone.at[me], send_sem=ssend.at[d], recv_sem=srecv.at[d],
            device_id=where_is(d), device_id_type=MESH,
        )

    def stat_go(d, c):
        stat_copy(d).start()
        return c

    def stat_wait(d, c):
        stat_copy(d).wait()
        return c

    def win_copy(kind, d):
        t = lax.rem(my + d, n_my)
        if kind == 0:
            src, dst, a = coarse, window.at[my, pl.ds(1, 2)], mx
        elif kind == 1:
            src, dst, a = coarse.at[pl.ds(0, 1)], window.at[my, pl.ds(3, 1)], mx - 1
        else:
            src, dst, a = coarse.at[pl.ds(1, 1)], window.at[my, pl.ds(0, 1)], mx + 1
        return pltpu.make_async_remote_copy(
            src_ref=src, dst_ref=dst, send_sem=wsend.at[kind, d], recv_sem=wrecv.at[kind, d],
            device_id=(a, t), device_id_type=MESH,
        )

    lax.fori_loop(1, n, stat_go, 0)
    low, high = mx > 0, mx < n_mx - 1
    for d in range(n_my):
        if d:
            win_copy(0, d).start()

        @pl.when(low)
        def _():
            win_copy(1, d).start()

        @pl.when(high)
        def _():
            win_copy(2, d).start()
    window[my, 1:3] = coarse[...]
    everyone[me] = stats[...]

    @pl.when(jnp.logical_not(low))
    def _():
        for j in range(n_my):
            window[j, 0] = jnp.zeros_like(window[j, 0])

    @pl.when(jnp.logical_not(high))
    def _():
        for j in range(n_my):
            window[j, 3] = jnp.zeros_like(window[j, 3])

    pad[...] = jnp.zeros_like(pad)
    group = wide_c // GROUPS
    same = (
        lax.broadcasted_iota(jnp.int32, (wide_c, wide_c), 0) // group
        == lax.broadcasted_iota(jnp.int32, (wide_c, wide_c), 1) // group
    ).astype(F32)
    for c in loads[1:]:
        c.wait()
    for d in range(n_my):
        if d:
            win_copy(0, d).wait()

        @pl.when(low)
        def _():
            win_copy(1, d).wait_send()
            win_copy(2, d).wait_recv()

        @pl.when(high)
        def _():
            win_copy(2, d).wait_send()
            win_copy(1, d).wait_recv()
    lax.fori_loop(1, n, stat_wait, 0)

    total = float(cells * group) * n
    sums = jnp.sum(everyone[...], axis=0)
    sums = jnp.concatenate([sums, jnp.zeros((6, wide_c), F32)], axis=0)
    sums = jnp.dot(sums, same, precision=lax.Precision.HIGHEST, preferred_element_type=F32) / total
    mean = sums[0:1]
    std = jnp.sqrt(sums[1:2] - mean * mean + norm_eps)
    g = gain[...]
    b = bias[...]
    for zw in range(4):
        for j in range(n_my):
            value = silu((window[j, zw] - mean) / std * g + b)
            if zw == 0:
                value = jnp.where(low, value, 0.0)
            if zw == 3:
                value = jnp.where(high, value, 0.0)
            for x in range(2):
                pad[1 + x, zw, 1 + 2 * j : 3 + 2 * j, :] = value[2 * x : 2 * x + 2]
    tall = 2 * n_my
    sums = jnp.zeros((4 * tall, part.shape[2]), F32)
    t = 0
    for dz in range(3):
        for dy in range(3):
            for dx in range(3):
                lhs = jnp.concatenate(
                    [pad[x + dx, z + dz, dy : dy + tall, :] for z in range(2) for x in range(2)],
                    axis=0,
                ).astype(BF)
                sums = sums + lax.dot_general(
                    lhs, weight[:, t * wide_c : (t + 1) * wide_c], (((1,), (1,)), ((), ())),
                    preferred_element_type=F32,
                )
                t += 1
    for j in range(n_my):
        for zx in range(4):
            part[j, 2 * zx : 2 * zx + 2, :] = sums[zx * tall + 2 * j : zx * tall + 2 * j + 2, :]
    copies = []
    for d in range(1, n_my):
        to = lax.rem(my + d, n_my)
        copies.append(
            pltpu.make_async_remote_copy(
                src_ref=part.at[to], dst_ref=result.at[my], send_sem=rsend.at[d],
                recv_sem=rrecv.at[d], device_id=(mx, to), device_id_type=MESH,
            )
        )
    for c in copies:
        c.start()
    result[my] = part[my]
    for c in copies:
        c.wait()

    whole = jnp.concatenate([result[j] for j in range(n_my)], axis=1)
    co = (whole + jnp.concatenate([coarse[0], coarse[1]], axis=0)).astype(BF)
    cof = co.astype(F32)
    for z in range(2):
        for y in range(2):
            q = z * 4 + y
            pair = jnp.concatenate([cof[q : q + 1], cof[q + 2 : q + 3]], axis=0)
            coarse_out[z, y] = pair.astype(BF)
    wide = jnp.dot(co, up[...], preferred_element_type=F32)
    for p in range(8):
        for q in range(cells):
            lifted[p * cells + q] = wide[q : q + 1, p * width : (p + 1) * width]
    pick = (
        lax.broadcasted_iota(jnp.int32, (chans, width), 0)
        == lax.broadcasted_iota(jnp.int32, (chans, width), 1) % chans
    )
    oc = octs[...]

    def join(j, c):
        row = jnp.where(pick, lifted[tgt[j]], 0.0)
        hi = row.astype(BF)
        lo = (row - hi.astype(F32)).astype(BF)
        both = jnp.dot(jnp.concatenate([hi, lo], axis=0), oc, preferred_element_type=F32)
        f = (level[j].astype(F32) + (both[:chans] + both[chans:])).astype(BF)
        level[j] = f
        ext[j] = silu(f.astype(F32)).astype(BF)
        return c

    lax.fori_loop(0, slots, join, 0, unroll=UNROLL)
    send_faces(1, ext)

    def second_done(j, value):
        f = value.astype(BF)
        level[j] = f
        ext2[j] = silu(f.astype(F32)).astype(BF)

    conv(1, level, ext, second_done)
    send_faces(2, ext2)

    def last_done(j, value):
        out[j] = value.astype(BF)

    conv(2, level, ext2, last_done)


def local(
    features, coords, counts, neighbours, fine_weights, down_weight, up_weight, norm_gain,
    norm_bias, coarse_weight,
):
    slots, chans, _ = features.shape
    n_mx, n_my = lax.axis_size("mx"), lax.axis_size("my")
    major, minor = lax.axis_index("mx"), lax.axis_index("my")
    cells = (RZ // 2) * (RY // 2) * (RX // 2)
    width = down_weight.shape[1]
    masks, pool, spread, octs = constants(chans)
    ids = jnp.arange(slots, dtype=jnp.int32)
    lin = ((coords[0] - major * RZ) * RY + coords[1] - minor * RY) * RX + coords[2]
    lin = jnp.where(ids < counts[0], lin, -1)
    hit = lin[None, :] == jnp.arange(RZ * RY * RX, dtype=jnp.int32)[:, None]
    slot_at = slots + jnp.sum(jnp.where(hit, ids - slots, 0), axis=1)
    n = n_mx * n_my
    sds = jax.ShapeDtypeStruct
    weight_t = coarse_weight.T
    held = [
        pltpu.VMEM(a.shape, a.dtype)
        for a in (octs, down_weight, up_weight, weight_t)
    ]
    ext = pltpu.VMEM((slots + 1 + 4 * NPOS, chans, VOL), BF)
    ext_small = pltpu.VMEM((slots, chans, VOL), BF)
    dma = pltpu.SemaphoreType.DMA
    scratch = held + [
        ext, ext,
        pltpu.VMEM((slots, chans, VOL), F32),
        ext_small,
        pltpu.VMEM((3, 4, NPOS // 2, chans, LANES), BF),
        pltpu.VMEM((3, 4, NPOS // 2, chans, LANES), BF),
        pltpu.VMEM((slots + 1, 8, chans), F32),
        pltpu.VMEM((8 * cells * 8, chans), F32),
        pltpu.VMEM((2, cells // 2, width), F32),
        pltpu.VMEM((2, width), F32),
        pltpu.VMEM((n_my, 4, cells // 2, width), F32),
        pltpu.VMEM((n, 2, width), F32),
        pltpu.VMEM((4, 4, -(-(2 * n_my + 2) // 8) * 8, width), F32),
        pltpu.VMEM((n_my, cells, coarse_weight.shape[1]), F32),
        pltpu.VMEM((n_my, cells, coarse_weight.shape[1]), F32),
        pltpu.VMEM((8 * cells, 1, 8 * chans), F32),
        pltpu.SMEM((6, slots), jnp.int32),
        pltpu.SMEM((slots,), jnp.int32),
        dma((4,)), dma((3, 4)), dma((3, 4)), dma((n,)), dma((n,)),
        dma((3, n_my)), dma((3, n_my)), dma((n_my,)), dma((n_my,)),
    ]
    fine, out = pl.pallas_call(
        functools.partial(level_kernel, slots, chans, cells),
        out_shape=(sds(features.shape, BF), sds((RZ // 2, RY // 2, RX // 2, width), BF)),
        in_specs=[SM] * 4 + [VM] * 7 + [pl.BlockSpec(memory_space=pl.ANY)] * 4,
        out_specs=(VM, VM),
        scratch_shapes=scratch,
        compiler_params=pltpu.CompilerParams(collective_id=0, has_side_effects=True),
    )(
        slot_at, coords, counts, neighbours, features, fine_weights, norm_gain[None, :],
        norm_bias[None, :], pool, spread, masks, octs, down_weight, up_weight, weight_t,
    )
    fine = jnp.where((ids < counts[0])[:, None, None], fine, jnp.zeros_like(fine))
    return fine, out


def solution(mesh):
    in_specs = (
        P(("mx", "my"), None, None),
        P(None, ("mx", "my")),
        P(("mx", "my")),
        P(None, ("mx", "my")),
        P(),
        P(),
        P(),
        P(),
        P(),
        P(None, "my"),
    )
    out_specs = (P(("mx", "my"), None, None), P("mx", "my", None, None))
    return jax.shard_map(local, mesh=mesh, in_specs=in_specs, out_specs=out_specs, check_vma=False)
```
